32 devices in a mesh: section: 16 (over z, y, x), dp: 2 (over core).
Axes of the slice: x: 2, y: 2, z: 4, core: 2. Of those that a mesh axis runs over, the one named last changes fastest.
Arguments:
- pipe_maps: bfloat16 [16, 2, 8, 32, 384], P('section', 'dp'), may hold values from -6 to 6
- fresh_maps: bfloat16 [3, 2, 8, 32, 384], P(None, 'dp'), may hold values from -6 to 6
- teacher_weight: bfloat16 [32, 3, 3, 384, 384], P('section'), may hold values from -0.109375 to 0.109375
- student_depth: float32 [32, 49, 384], P('section'), may hold values from -0.875 to 0.875
- student_point: bfloat16 [32, 384, 384], P('section'), may hold values from -0.3125 to 0.3125
Outputs:
- final_maps: bfloat16 [16, 2, 8, 32, 384], P('section', 'dp')
- point_grad: float32 [32, 384, 384], P('section', None, 'dp')
- depth_grad: float32 [32, 49, 384], P('section', None, 'dp')
The draws below stay inside these ranges and needn't reach their ends.
All inputs are finite; a program needn't handle non-finite values.
Results may differ from the reference program's by a relative error of at most 0.012.
Values may be sent and summed in bfloat16 or wider, within the bound.
A program may use at most 128 MiB of HBM per device.

```python
import jax
import jax.numpy as jnp
from jax import lax

CHANNELS = 384
MAP_H = 8
MAP_W = 32
TAPS = 49
TICKS = 4
BATCH = 2
SECTIONS = 16


def block_scale(rng, extent, shards, smallest, largest):
    gain, own = 1.0, jax.random.fold_in(rng, 6)
    for position, blocks in shards:
        steps = jnp.exp(jax.random.uniform(jax.random.fold_in(own, position), (blocks,), jnp.float32, smallest / len(shards), largest / len(shards)))
        gain = gain * jnp.repeat(steps, extent[position] // blocks).reshape([-1 if axis == position else 1 for axis in range(len(extent))])
    return gain


def noise(stream_key, shape, deviation, limit, split=(), kind=jnp.bfloat16):
    result = deviation * jax.random.normal(stream_key, shape, jnp.float32)
    if split:
        result = result * block_scale(stream_key, shape, split, -0.22, 0.18)
    return jnp.clip(result, -limit, limit).astype(kind)


def setup_inputs(seed: int = 0) -> dict:
    streams_of = jax.random.split(jax.random.key(seed), 6)
    return {
        "pipe_maps": noise(streams_of[0], (SECTIONS, BATCH, MAP_H, MAP_W, CHANNELS), 1.0, 6.0, ((0, 16), (1, 2))),
        "fresh_maps": noise(streams_of[1], (TICKS - 1, BATCH, MAP_H, MAP_W, CHANNELS), 1.0, 6.0, ((1, 2),)),
        "teacher_weight": noise(streams_of[2], (2 * SECTIONS, 3, 3, CHANNELS, CHANNELS), (9 * CHANNELS) ** -0.5, 0.109375, ((0, 16),)),
        "student_depth": noise(streams_of[3], (2 * SECTIONS, TAPS, CHANNELS), TAPS ** -0.5, 0.875, ((0, 16),), jnp.float32),
        "student_point": noise(streams_of[4], (2 * SECTIONS, CHANNELS, CHANNELS), CHANNELS ** -0.5, 0.3125, ((0, 16),)),
    }


def teacher_conv(inmap, kernel):
    batch, height, width, chans = inmap.shape
    padded = jnp.pad(inmap, ((0, 0), (1, 1), (1, 1), (0, 0)))
    total = jnp.zeros((batch * height * width, kernel.shape[-1]), jnp.float32)
    for row in range(3):
        for col in range(3):
            window = padded[:, row:row + height, col:col + width, :].reshape(-1, chans)
            total = total + jnp.dot(window, kernel[row, col], preferred_element_type=jnp.float32)
    return total.reshape(batch, height, width, kernel.shape[-1])

def teacher_pass(inmap, kernels):
    hidden = jnp.maximum(teacher_conv(inmap, kernels[0]), 0.0).astype(jnp.bfloat16)
    summed = inmap.astype(jnp.float32) + teacher_conv(hidden, kernels[1])
    return (0.8 * summed).astype(jnp.bfloat16)

def depth_conv(inmap, taps):
    height, width = (inmap.shape[1], inmap.shape[2])
    padded = jnp.pad(inmap, ((0, 0), (3, 3), (3, 3), (0, 0)))
    total = jnp.zeros(inmap.shape, jnp.float32)
    for row in range(7):
        for col in range(7):
            total = total + padded[:, row:row + height, col:col + width, :] * taps[row * 7 + col]
    return total

def point_apply(gelled, weight):
    chans = weight.shape[0]
    flat = jnp.dot(gelled.reshape(-1, chans), weight, preferred_element_type=jnp.float32)
    return flat.reshape(gelled.shape)

def weight_grad(gelled, upstream):
    chans = gelled.shape[-1]
    return lax.dot_general(gelled.reshape(-1, chans), upstream.reshape(-1, chans), (((0,), (0,)), ((), ())), preferred_element_type=jnp.float32)

def block_back(start_map, act_map, upstream, taps, weight):
    up_bf = upstream.astype(jnp.bfloat16)
    gelled = jax.nn.gelu(act_map).astype(jnp.bfloat16)
    point_part = weight_grad(gelled, up_bf)
    dgel = point_apply(up_bf, weight.T)
    dact = jax.vjp(jax.nn.gelu, act_map)[1](dgel)[0]
    back_map, back_taps = jax.vjp(depth_conv, start_map, taps)[1](dact)
    return (point_part, back_taps, upstream + back_map)

def student_grads(inmap, teach, depth, point):
    area = inmap.shape[1] * inmap.shape[2]
    start_zero = inmap.astype(jnp.float32)
    act_zero = depth_conv(start_zero, depth[0])
    start_one = start_zero + point_apply(jax.nn.gelu(act_zero).astype(jnp.bfloat16), point[0])
    act_one = depth_conv(start_one, depth[1])
    final_map = start_one + point_apply(jax.nn.gelu(act_one).astype(jnp.bfloat16), point[1])
    resid = (final_map - teach.astype(jnp.float32)) * (4.0 / area)
    point_one, taps_one, back_one = block_back(start_one, act_one, resid, depth[1], point[1])
    point_zero, taps_zero, back_zero = block_back(start_zero, act_zero, back_one, depth[0], point[0])
    return (jnp.stack([point_zero, point_one]), jnp.stack([taps_zero, taps_one]))

def reference(pipe_maps, fresh_maps, teacher_weight, student_depth, student_point):
    chans = teacher_weight.shape[-1]
    section_count = pipe_maps.shape[0]
    kernels = teacher_weight.reshape(section_count, 2, 3, 3, chans, chans)
    depth = student_depth.reshape(section_count, 2, student_depth.shape[1], chans)
    point = student_point.reshape(section_count, 2, chans, chans)
    current = pipe_maps
    point_total = jnp.zeros((section_count, 2, chans, chans), jnp.float32)
    depth_total = jnp.zeros((section_count, 2, student_depth.shape[1], chans), jnp.float32)

    def per_section(packed):
        inmap, kern, taps, weight = packed
        teach = teacher_pass(inmap, kern)
        point_part, depth_part = student_grads(inmap, teach, taps, weight)
        return (teach, point_part, depth_part)
    teach_all = current
    for tick_index in range(TICKS):
        teach_all, point_part, depth_part = lax.map(per_section, (current, kernels, depth, point))
        point_total = point_total + point_part
        depth_total = depth_total + depth_part
        if tick_index + 1 < TICKS:
            current = jnp.concatenate([fresh_maps[tick_index][None], teach_all[:-1]], axis=0)
    return (teach_all, point_total.reshape(2 * section_count, chans, chans), depth_total.reshape(2 * section_count, student_depth.shape[1], chans))
```

```python
import functools

import jax
import jax.numpy as jnp
from jax import lax
from jax.experimental import pallas as pl
from jax.experimental.pallas import tpu as pltpu
from jax.sharding import PartitionSpec as P

LANES = 128
F32 = jnp.float32
BF16 = jnp.bfloat16
NT = (((1,), (1,)), ((), ()))


def gather_windows(vals, win_ref, width, height):
    chans = vals.shape[-1]
    rows = width * height
    h_of = lax.rem(lax.broadcasted_iota(jnp.int32, (rows, chans), 0), height)
    zero = jnp.zeros((height, chans), F32)
    cube = vals.reshape(width, height, chans)
    for row in range(3):
        dy = row - 1
        if dy:
            moved = pltpu.roll(cube, (-dy) % height, 1).reshape(rows, chans)
            moved = jnp.where((h_of + dy >= 0) & (h_of + dy < height), moved, 0.0)
        else:
            moved = vals
        for col in range(3):
            if col == 0:
                part = jnp.concatenate([zero, moved[: rows - height]], axis=0)
            elif col == 2:
                part = jnp.concatenate([moved[height:], zero], axis=0)
            else:
                part = moved
            tap = row * 3 + col
            win_ref[:, tap * chans : (tap + 1) * chans] = part.astype(BF16)


def teacher_kernel(width, height, lead_ref, fresh_ref, relay_ref, weight_ref, teach_ref, cur_ref, win_ref):
    lead = lead_ref[0] == 1
    current = jnp.where(lead, fresh_ref[...].astype(F32), relay_ref[...].astype(F32))
    cur_ref[...] = current.astype(BF16)
    gather_windows(current, win_ref, width, height)
    hidden = jnp.dot(win_ref[...], weight_ref[0], preferred_element_type=F32)
    gather_windows(jnp.maximum(hidden, 0.0), win_ref, width, height)
    second = jnp.dot(win_ref[...], weight_ref[1], preferred_element_type=F32)
    teach_ref[...] = (0.8 * (current + second)).astype(BF16)


def teacher(lead, fresh, relay, weight, width, height):
    rows, chans = fresh.shape
    vmem = pl.BlockSpec(memory_space=pltpu.VMEM)
    return pl.pallas_call(
        functools.partial(teacher_kernel, width, height),
        out_shape=(jax.ShapeDtypeStruct((rows, chans), BF16),) * 2,
        in_specs=[pl.BlockSpec(memory_space=pltpu.SMEM), vmem, vmem, vmem],
        out_specs=(vmem, vmem),
        scratch_shapes=[pltpu.VMEM((rows, 9 * chans), BF16)],
        compiler_params=pltpu.CompilerParams(vmem_limit_bytes=24 << 20),
        cost_estimate=pl.CostEstimate(
            flops=2 * 2 * 9 * rows * chans * chans, bytes_accessed=weight.size * 2, transcendentals=0
        ),
        name="teacher",
    )(lead, fresh, relay, weight)


def spread(cube, out_ref, block):
    width, height, _ = cube.shape
    h_of = lax.broadcasted_iota(jnp.int32, cube.shape, 1)
    for row in range(7):
        dy = row - 3
        moved = cube
        if dy:
            moved = pltpu.roll(cube, (-dy) % height, 1)
            moved = jnp.where((h_of + dy >= 0) & (h_of + dy < height), moved, 0.0)
        out_ref[block, row, 3 : 3 + width] = moved


def clear_edges(out_ref, width):
    edge = jnp.zeros(out_ref.shape[:2] + (3,) + out_ref.shape[3:], F32)
    out_ref[:, :, 0:3] = edge
    out_ref[:, :, 3 + width : 6 + width] = edge


def tap_sum(src_ref, block, taps_ref, which, start, count, flip):
    lanes = slice(block * LANES, (block + 1) * LANES)
    height = src_ref.shape[3]
    total = jnp.zeros((count, height, LANES), F32)
    for row in range(7):
        strip = src_ref[block, row, pl.ds(start, count + 6)]
        for col in range(7):
            tap = row * 7 + col
            tap = 48 - tap if flip else tap
            coef = jnp.broadcast_to(taps_ref[which, tap : tap + 1, lanes], (height, LANES))
            total = total + strip[col : col + count] * coef[None]
    return total


def gelu_pair(act):
    root = 0.7978845608028654
    square = act * act
    tanh = jnp.tanh(root * (act + 0.044715 * square * act))
    half = 0.5 * (1.0 + tanh)
    slope = half + 0.5 * act * (1.0 - tanh * tanh) * (root * (1.0 + 3.0 * 0.044715 * square))
    return act * half, slope


def student_kernel(
    width, height, step, cur_ref, teach_ref, taps_ref, point_ref,
    gel_ref, grad_ref, dk_ref, src0, src1, src2, slope0, slope1, dact, resid_ref,
):
    rows, chans = cur_ref.shape
    blocks = chans // LANES
    chunks = width // step
    srcs, slopes = (src0, src1), (slope0, slope1)
    area = width * height

    def lanes(block):
        return slice(block * LANES, (block + 1) * LANES)

    for ref in (src0, src1, src2):
        clear_edges(ref, width)
    for block in range(blocks):
        spread(cur_ref[:, lanes(block)].astype(F32).reshape(width, height, LANES), src0, block)

    def forward(which):
        def chunk(index, carry):
            start = index * step
            for block in range(blocks):
                act = tap_sum(srcs[which], block, taps_ref, which, start, step, False)
                gel, slope = gelu_pair(act)
                slopes[which][block, pl.ds(start, step)] = slope
                at = pl.ds(pl.multiple_of(start * height, step * height), step * height)
                gel_ref[which, at, lanes(block)] = gel.reshape(step * height, LANES).astype(BF16)
            return carry

        lax.fori_loop(0, chunks, chunk, 0)
        return jnp.dot(gel_ref[which], point_ref[which], preferred_element_type=F32)

    first = forward(0)
    for block in range(blocks):
        u_one = first[:, lanes(block)] + cur_ref[:, lanes(block)].astype(F32)
        spread(u_one.reshape(width, height, LANES), src1, block)
    second = forward(1)
    for block in range(blocks):
        u_one = src1[block, 3, 3 : 3 + width].reshape(rows, LANES)
        diff = u_one + second[:, lanes(block)] - teach_ref[:, lanes(block)].astype(F32)
        resid = diff * (4.0 / area)
        resid_ref[block] = resid.reshape(width, height, LANES)
        grad_ref[1, :, lanes(block)] = resid.astype(BF16)

    def taps_grad(which):
        def over_rows(row, carry):
            for block in range(blocks):
                sums = [jnp.zeros((height, LANES), F32)] * 7
                for index in range(chunks):
                    strip = srcs[which][block, row, pl.ds(index * step, step + 6)]
                    part = dact[block, pl.ds(index * step, step)]
                    for col in range(7):
                        sums[col] = sums[col] + jnp.sum(strip[col : col + step] * part, axis=0)
                for col in range(7):
                    dk_ref[which, block, row, col : col + 1, :] = jnp.sum(sums[col], axis=0, keepdims=True)
                dk_ref[which, block, row, 7:8, :] = jnp.zeros((1, LANES), F32)
            return carry

        lax.fori_loop(0, 7, over_rows, 0)

    def back_point(which):
        dgel = lax.dot_general(grad_ref[which], point_ref[which], NT, preferred_element_type=F32)
        for block in range(blocks):
            dact[block] = dgel[:, lanes(block)].reshape(width, height, LANES) * slopes[which][block]

    back_point(1)
    for block in range(blocks):
        spread(dact[block], src2, block)

    def chunk_back(index, carry):
        start = index * step
        for block in range(blocks):
            back = tap_sum(src2, block, taps_ref, 1, start, step, True)
            back = back + resid_ref[block, pl.ds(start, step)]
            at = pl.ds(pl.multiple_of(start * height, step * height), step * height)
            grad_ref[0, at, lanes(block)] = back.reshape(step * height, LANES).astype(BF16)
        return carry

    lax.fori_loop(0, chunks, chunk_back, 0)
    taps_grad(1)
    back_point(0)
    taps_grad(0)


def student(current, teach, taps, point, width, height):
    rows, chans = current.shape
    blocks = chans // LANES
    vmem = pl.BlockSpec(memory_space=pltpu.VMEM)
    spread_shape = pltpu.VMEM((blocks, 7, width + 6, height, LANES), F32)
    map_shape = pltpu.VMEM((blocks, width, height, LANES), F32)
    return pl.pallas_call(
        functools.partial(student_kernel, width, height, width // 2),
        out_shape=(
            jax.ShapeDtypeStruct((2, rows, chans), BF16),
            jax.ShapeDtypeStruct((2, rows, chans), BF16),
            jax.ShapeDtypeStruct((2, blocks, 7, 8, LANES), F32),
        ),
        in_specs=[vmem] * 4,
        out_specs=(vmem,) * 3,
        scratch_shapes=[spread_shape] * 3 + [map_shape] * 4,
        compiler_params=pltpu.CompilerParams(vmem_limit_bytes=32 << 20),
        cost_estimate=pl.CostEstimate(
            flops=10_000_000_000, bytes_accessed=8 * rows * chans, transcendentals=0
        ),
        name="student",
    )(current, teach, taps, point)


def body(pipe_maps, fresh_maps, teacher_weight, student_depth, student_point):
    _, _, height, width, chans = pipe_maps.shape
    rows = height * width
    blocks = chans // LANES
    lead = (lax.axis_index("section") == 0).astype(jnp.int32).reshape(1)
    sections = lax.axis_size("section")
    route = [(i, i + 1) for i in range(sections - 1)]

    def to_rows(maps):
        return jnp.swapaxes(maps, -3, -2).reshape(maps.shape[:-3] + (rows, chans))

    relay = to_rows(pipe_maps[0, 0])
    fresh = to_rows(fresh_maps[:, 0])
    weight = teacher_weight.reshape(2, 9 * chans, chans)
    ticks = fresh_maps.shape[0] + 1
    gels, grads, depth_total = [], [], None
    teach = relay
    for tick in range(ticks):
        mine = relay if tick == 0 else fresh[tick - 1]
        teach, current = teacher(lead, mine, relay, weight, width, height)
        if tick + 1 < ticks:
            relay = lax.ppermute(teach, "section", route)
        gel, grad, part = student(current, teach, student_depth, student_point, width, height)
        gels.append(gel)
        grads.append(grad)
        depth_total = part if depth_total is None else depth_total + part
    gel_all = jnp.concatenate(gels, axis=1)
    grad_all = jnp.concatenate(grads, axis=1)
    point_total = [
        lax.dot_general(grad_all[b], gel_all[b], (((0,), (0,)), ((), ())), preferred_element_type=F32)
        for b in range(2)
    ]
    depth_rows = depth_total[:, :, :, :7].transpose(1, 4, 0, 2, 3).reshape(chans, 98)
    packed = jnp.concatenate(point_total + [depth_rows], axis=1)
    parties = lax.axis_size("dp")
    share = chans // parties
    me = lax.axis_index("dp")
    total = lax.dynamic_slice_in_dim(packed, me * share, share, 0)
    for hop in range(1, parties):
        out = lax.dynamic_slice_in_dim(packed, lax.rem(me + hop, parties) * share, share, 0)
        pairs = [(i, (i + hop) % parties) for i in range(parties)]
        total = total + lax.ppermute(out.astype(BF16), "dp", pairs).astype(F32)
    point_grad = jnp.stack([total[:, b * chans : (b + 1) * chans].T for b in range(2)])
    depth_grad = total[:, 2 * chans :].T.reshape(2, 49, share)
    final = jnp.swapaxes(teach.reshape(width, height, chans), 0, 1)[None, None]
    return final, point_grad, depth_grad


def solution(mesh):
    placed = (
        P("section", "dp", None, None, None),
        P(None, "dp", None, None, None),
        P("section", None, None, None, None),
        P("section", None, None),
        P("section", None, None),
    )
    return jax.shard_map(
        body,
        mesh=mesh,
        in_specs=placed,
        out_specs=(
            P("section", "dp", None, None, None),
            P("section", None, "dp"),
            P("section", None, "dp"),
        ),
        check_vma=False,
    )
```

```python
import functools

import jax
import jax.numpy as jnp
from jax import lax
from jax.experimental import pallas as pl
from jax.experimental.pallas import tpu as pltpu
from jax.sharding import PartitionSpec as P

LANES = 128
F32 = jnp.float32
BF16 = jnp.bfloat16
NT = (((1,), (1,)), ((), ()))


def gather_windows(vals, win_ref, height):
    rows, chans = vals.shape
    pair = 2 * height
    h_of = lax.rem(lax.broadcasted_iota(jnp.int32, (rows, chans), 0), height)
    zero = jnp.zeros((height, chans), F32)
    cube = vals.reshape(rows // height, height, chans)
    for row in range(3):
        dy = row - 1
        moved = vals
        if dy:
            moved = pltpu.roll(cube, (-dy) % height, 1).reshape(rows, chans)
            moved = jnp.where((h_of + dy >= 0) & (h_of + dy < height), moved, 0.0)
        for col in range(3):
            if col == 0:
                part = jnp.concatenate([zero, moved[rows - pair : rows - height], moved[: rows - pair]], axis=0)
            elif col == 2:
                part = jnp.concatenate([moved[pair:], moved[height:pair], zero], axis=0)
            else:
                part = moved
            tap = row * 3 + col
            win_ref[:, tap * chans : (tap + 1) * chans] = part.astype(BF16)


def teacher_kernel(height, lead_ref, fresh_ref, relay_ref, weight_ref, teach_ref, cur_ref, win_ref):
    lead = lead_ref[0] == 1
    current = jnp.where(lead, fresh_ref[...].astype(F32), relay_ref[...].astype(F32))
    cur_ref[...] = current.astype(BF16)
    gather_windows(current, win_ref, height)
    hidden = jnp.dot(win_ref[...], weight_ref[0], preferred_element_type=F32)
    gather_windows(jnp.maximum(hidden, 0.0), win_ref, height)
    second = jnp.dot(win_ref[...], weight_ref[1], preferred_element_type=F32)
    teach_ref[...] = (0.8 * (current + second)).astype(BF16)


def teacher(lead, fresh, relay, weight, height):
    rows, chans = fresh.shape
    vmem = pl.BlockSpec(memory_space=pltpu.VMEM)
    return pl.pallas_call(
        functools.partial(teacher_kernel, height),
        out_shape=(jax.ShapeDtypeStruct((rows, chans), BF16),) * 2,
        in_specs=[pl.BlockSpec(memory_space=pltpu.SMEM), vmem, vmem, vmem],
        out_specs=(vmem, vmem),
        scratch_shapes=[pltpu.VMEM((rows, 9 * chans), BF16)],
        compiler_params=pltpu.CompilerParams(vmem_limit_bytes=24 << 20),
        cost_estimate=pl.CostEstimate(
            flops=2 * 2 * 9 * rows * chans * chans, bytes_accessed=weight.size * 2, transcendentals=0
        ),
        name="teacher",
    )(lead, fresh, relay, weight)


def spread(vals, out_ref, block, height):
    pair = vals.reshape(-1, 2 * height, LANES)
    low, high = pair[:, :height], pair[:, height:]
    h_of = lax.broadcasted_iota(jnp.int32, low.shape, 1)
    zero = jnp.zeros((3, height, LANES), F32)
    for row in range(7):
        dy = row - 3
        one, two = low, high
        if dy:
            keep = (h_of + dy >= 0) & (h_of + dy < height)
            one = jnp.where(keep, pltpu.roll(low, (-dy) % height, 1), 0.0)
            two = jnp.where(keep, pltpu.roll(high, (-dy) % height, 1), 0.0)
        left = jnp.concatenate([zero, one, two[:3]], axis=0)
        right = jnp.concatenate([one[-3:], two, zero], axis=0)
        out_ref[block, row] = jnp.concatenate([left, right], axis=1).astype(BF16)


def tap_sum(src_ref, block, taps_ref, which, start, count, flip):
    total, held = None, None
    for row in range(7):
        strip = src_ref[block, row, pl.ds(start, count + 6)]
        terms = []
        for col in range(7):
            tap = row * 7 + col
            tap = 48 - tap if flip else tap
            terms.append(strip[col : col + count] * taps_ref[which, block, tap][None])
        while len(terms) > 1:
            terms = [sum(terms[i + 1 : i + 2], terms[i]) for i in range(0, len(terms), 2)]
        if held is None and row < 6:
            held = terms[0]
            continue
        part = terms[0] if held is None else held + terms[0]
        held = None
        total = part.astype(F32) if total is None else total + part.astype(F32)
    return total


def gelu_pair(act):
    root = 0.7978845608028654
    square = act * act
    tanh = jnp.tanh(root * (act + 0.044715 * square * act))
    half = 0.5 * (1.0 + tanh)
    slope = half + 0.5 * act * (1.0 - tanh * tanh) * (root * (1.0 + 3.0 * 0.044715 * square))
    return act * half, slope


def student_kernel(
    height, step, cur_ref, teach_ref, taps_ref, point_ref,
    gel_ref, grad_ref, dk_ref, src0, src1, src2, slope0, slope1, dact, u_one_ref, resid_ref,
):
    rows, chans = cur_ref.shape
    blocks = chans // LANES
    pair = 2 * height
    chunks = rows // (pair * step)
    srcs, slopes = (src0, src1), (slope0, slope1)

    def lanes(block):
        return slice(block * LANES, (block + 1) * LANES)

    def span(index):
        return pl.ds(pl.multiple_of(index * step * pair, step * pair), step * pair)

    for block in range(blocks):
        spread(cur_ref[:, lanes(block)].astype(F32), src0, block, height)

    def forward(which):
        def chunk(index, carry):
            for block in range(blocks):
                act = tap_sum(srcs[which], block, taps_ref, which, index * step, step, False)
                gel, slope = gelu_pair(act.reshape(step * pair, LANES))
                slopes[which][span(index), lanes(block)] = slope
                gel_ref[which, span(index), lanes(block)] = gel.astype(BF16)
            return carry

        lax.fori_loop(0, chunks, chunk, 0)
        return jnp.dot(gel_ref[which], point_ref[which], preferred_element_type=F32)

    u_one_ref[...] = forward(0) + cur_ref[...].astype(F32)
    for block in range(blocks):
        spread(u_one_ref[:, lanes(block)], src1, block, height)
    diff = forward(1) + u_one_ref[...] - teach_ref[...].astype(F32)
    resid = diff * (4.0 / rows)
    resid_ref[...] = resid
    grad_ref[1] = resid.astype(BF16)

    def taps_grad(which):
        def over_rows(row, carry):
            for block in range(blocks):
                strip = srcs[which][block, row]
                part = dact[:, lanes(block)].reshape(-1, pair, LANES)
                count = part.shape[0]
                for col in range(7):
                    prod = strip[col : col + count] * part
                    size = count
                    while size > 1:
                        size //= 2
                        prod = prod[:size] + prod[size:]
                    line = jnp.sum(prod[0].astype(F32), axis=0, keepdims=True)
                    dk_ref[which, block, row, col : col + 1, :] = line
                dk_ref[which, block, row, 7:8, :] = jnp.zeros((1, LANES), F32)
            return carry

        lax.fori_loop(0, 7, over_rows, 0)

    def back_point(which):
        dgel = lax.dot_general(grad_ref[which], point_ref[which], NT, preferred_element_type=F32)
        return dgel * slopes[which][...]

    dact_one = back_point(1)
    dact[...] = dact_one.astype(BF16)
    for block in range(blocks):
        spread(dact_one[:, lanes(block)], src2, block, height)

    def chunk_back(index, carry):
        for block in range(blocks):
            back = tap_sum(src2, block, taps_ref, 1, index * step, step, True)
            back = back.reshape(step * pair, LANES) + resid_ref[span(index), lanes(block)]
            grad_ref[0, span(index), lanes(block)] = back.astype(BF16)
        return carry

    lax.fori_loop(0, chunks, chunk_back, 0)
    taps_grad(1)
    dact[...] = back_point(0).astype(BF16)
    taps_grad(0)


def student(current, teach, taps, point, height):
    rows, chans = current.shape
    blocks = chans // LANES
    half = rows // (2 * height)
    vmem = pl.BlockSpec(memory_space=pltpu.VMEM)
    spread_shape = pltpu.VMEM((blocks, 7, half + 6, 2 * height, LANES), BF16)
    map_shape = pltpu.VMEM((rows, chans), F32)
    return pl.pallas_call(
        functools.partial(student_kernel, height, half // 2),
        out_shape=(
            jax.ShapeDtypeStruct((2, rows, chans), BF16),
            jax.ShapeDtypeStruct((2, rows, chans), BF16),
            jax.ShapeDtypeStruct((2, blocks, 7, 8, LANES), F32),
        ),
        in_specs=[vmem] * 4,
        out_specs=(vmem,) * 3,
        scratch_shapes=[spread_shape] * 3
        + [map_shape] * 2
        + [pltpu.VMEM((rows, chans), BF16)]
        + [map_shape] * 2,
        compiler_params=pltpu.CompilerParams(vmem_limit_bytes=32 << 20),
        cost_estimate=pl.CostEstimate(
            flops=10_000_000_000, bytes_accessed=8 * rows * chans, transcendentals=0
        ),
        name="student",
    )(current, teach, taps, point)


def body(pipe_maps, fresh_maps, teacher_weight, student_depth, student_point):
    _, _, height, width, chans = pipe_maps.shape
    rows = height * width
    blocks = chans // LANES
    lead = (lax.axis_index("section") == 0).astype(jnp.int32).reshape(1)
    sections = lax.axis_size("section")
    route = [(i, i + 1) for i in range(sections - 1)]

    def to_rows(maps):
        front = maps.shape[:-3]
        split = maps.reshape(front + (height, 2, width // 2, chans))
        return jnp.swapaxes(split, -4, -2).reshape(front + (rows, chans))

    relay = to_rows(pipe_maps[0, 0])
    fresh = to_rows(fresh_maps[:, 0])
    weight = teacher_weight.reshape(2, 9 * chans, chans)
    taps = student_depth.astype(BF16).reshape(2, -1, blocks, 1, LANES).swapaxes(1, 2)
    taps = jnp.broadcast_to(taps, taps.shape[:3] + (2 * height, LANES))
    ticks = fresh_maps.shape[0] + 1
    gels, grads, depth_total = [], [], None
    teach = relay
    for tick in range(ticks):
        mine = relay if tick == 0 else fresh[tick - 1]
        teach, current = teacher(lead, mine, relay, weight, height)
        if tick + 1 < ticks:
            relay = lax.ppermute(teach, "section", route)
        gel, grad, part = student(current, teach, taps, student_point, height)
        gels.append(gel)
        grads.append(grad)
        depth_total = part if depth_total is None else depth_total + part
    gel_all = jnp.concatenate(gels, axis=1)
    grad_all = jnp.concatenate(grads, axis=1)
    point_total = [
        lax.dot_general(grad_all[b], gel_all[b], (((0,), (0,)), ((), ())), preferred_element_type=F32)
        for b in range(2)
    ]
    depth_rows = depth_total[:, :, :, :7].transpose(1, 4, 0, 2, 3).reshape(chans, 98)
    packed = jnp.concatenate(point_total + [depth_rows], axis=1)
    parties = lax.axis_size("dp")
    share = chans // parties
    me = lax.axis_index("dp")
    total = lax.dynamic_slice_in_dim(packed, me * share, share, 0)
    for hop in range(1, parties):
        out = lax.dynamic_slice_in_dim(packed, lax.rem(me + hop, parties) * share, share, 0)
        pairs = [(i, (i + hop) % parties) for i in range(parties)]
        total = total + lax.ppermute(out.astype(BF16), "dp", pairs).astype(F32)
    point_grad = jnp.stack([total[:, b * chans : (b + 1) * chans].T for b in range(2)])
    depth_grad = total[:, 2 * chans :].T.reshape(2, 49, share)
    final = jnp.swapaxes(teach.reshape(width // 2, 2, height, chans), 0, 2)
    final = final.reshape(1, 1, height, width, chans)
    return final, point_grad, depth_grad


def solution(mesh):
    placed = (
        P("section", "dp", None, None, None),
        P(None, "dp", None, None, None),
        P("section", None, None, None, None),
        P("section", None, None),
        P("section", None, None),
    )
    return jax.shard_map(
        body,
        mesh=mesh,
        in_specs=placed,
        out_specs=(
            P("section", "dp", None, None, None),
            P("section", None, "dp"),
            P("section", None, "dp"),
        ),
        check_vma=False,
    )
```

```python
import functools

import jax
import jax.numpy as jnp
from jax import lax
from jax.experimental import pallas as pl
from jax.experimental.pallas import tpu as pltpu
from jax.sharding import PartitionSpec as P

LANES = 128
F32 = jnp.float32
BF16 = jnp.bfloat16
NT = (((1,), (1,)), ((), ()))


def gather_windows(vals, win_ref, height):
    rows, chans = vals.shape
    pair = 2 * height
    h_of = lax.rem(lax.broadcasted_iota(jnp.int32, (rows, chans), 0), height)
    zero = jnp.zeros((height, chans), F32)
    cube = vals.reshape(rows // height, height, chans)
    for row in range(3):
        dy = row - 1
        moved = vals
        if dy:
            moved = pltpu.roll(cube, (-dy) % height, 1).reshape(rows, chans)
            moved = jnp.where((h_of + dy >= 0) & (h_of + dy < height), moved, 0.0)
        for col in range(3):
            if col == 0:
                part = jnp.concatenate([zero, moved[rows - pair : rows - height], moved[: rows - pair]], axis=0)
            elif col == 2:
                part = jnp.concatenate([moved[pair:], moved[height:pair], zero], axis=0)
            else:
                part = moved
            tap = row * 3 + col
            win_ref[:, tap * chans : (tap + 1) * chans] = part.astype(BF16)


def teacher_kernel(height, lead_ref, fresh_ref, relay_ref, weight_ref, teach_ref, cur_ref, win_ref):
    lead = lead_ref[0] == 1
    current = jnp.where(lead, fresh_ref[...].astype(F32), relay_ref[...].astype(F32))
    cur_ref[...] = current.astype(BF16)
    gather_windows(current, win_ref, height)
    hidden = jnp.dot(win_ref[...], weight_ref[0], preferred_element_type=F32)
    gather_windows(jnp.maximum(hidden, 0.0), win_ref, height)
    second = jnp.dot(win_ref[...], weight_ref[1], preferred_element_type=F32)
    teach_ref[...] = (0.8 * (current + second)).astype(BF16)


def teacher(lead, fresh, relay, weight, height):
    rows, chans = fresh.shape
    vmem = pl.BlockSpec(memory_space=pltpu.VMEM)
    return pl.pallas_call(
        functools.partial(teacher_kernel, height),
        out_shape=(jax.ShapeDtypeStruct((rows, chans), BF16),) * 2,
        in_specs=[pl.BlockSpec(memory_space=pltpu.SMEM), vmem, vmem, vmem],
        out_specs=(vmem, vmem),
        scratch_shapes=[pltpu.VMEM((rows, 9 * chans), BF16)],
        compiler_params=pltpu.CompilerParams(vmem_limit_bytes=24 << 20),
        cost_estimate=pl.CostEstimate(
            flops=2 * 2 * 9 * rows * chans * chans, bytes_accessed=weight.size * 2, transcendentals=0
        ),
        name="teacher",
    )(lead, fresh, relay, weight)


def spread(vals, out_ref, block, height):
    pair = vals.reshape(-1, 2 * height, LANES)
    low, high = pair[:, :height], pair[:, height:]
    h_of = lax.broadcasted_iota(jnp.int32, low.shape, 1)
    zero = jnp.zeros((3, height, LANES), F32)
    for row in range(7):
        dy = row - 3
        one, two = low, high
        if dy:
            keep = (h_of + dy >= 0) & (h_of + dy < height)
            one = jnp.where(keep, pltpu.roll(low, (-dy) % height, 1), 0.0)
            two = jnp.where(keep, pltpu.roll(high, (-dy) % height, 1), 0.0)
        left = jnp.concatenate([zero, one, two[:3]], axis=0)
        right = jnp.concatenate([one[-3:], two, zero], axis=0)
        out_ref[block, row] = jnp.concatenate([left, right], axis=1)


def columns(block):
    return pl.ds(pl.multiple_of(block * LANES, LANES), LANES)


def tap_sum(src_ref, block, taps_ref, which, start, count, flip):
    total, held = None, None
    for row in range(7):
        strip = src_ref[block, row, pl.ds(start, count + 6)].astype(BF16)
        terms = []
        for col in range(7):
            tap = row * 7 + col
            tap = 48 - tap if flip else tap
            coef = jnp.broadcast_to(taps_ref[which, tap : tap + 1, columns(block)], strip.shape[1:])
            terms.append(strip[col : col + count] * coef.astype(BF16)[None])
        while len(terms) > 1:
            terms = [sum(terms[i + 1 : i + 2], terms[i]) for i in range(0, len(terms), 2)]
        if held is None and row < 6:
            held = terms[0]
            continue
        part = terms[0] if held is None else held + terms[0]
        held = None
        total = part.astype(F32) if total is None else total + part.astype(F32)
    return total


def gelu_pair(act):
    root = 0.7978845608028654
    square = act * act
    tanh = jnp.tanh(root * (act + 0.044715 * square * act))
    half = 0.5 * (1.0 + tanh)
    slope = half + 0.5 * act * (1.0 - tanh * tanh) * (root * (1.0 + 3.0 * 0.044715 * square))
    return act * half, slope


def student_kernel(
    height, step, cur_ref, teach_ref, taps_ref, point_ref,
    gel_ref, grad_ref, dk_ref, src0, src1, src2, slope0, slope1, dact, u_one_ref, resid_ref,
):
    rows, chans = cur_ref.shape
    blocks = chans // LANES
    pair = 2 * height
    chunks = rows // (pair * step)
    srcs, slopes = (src0, src1), (slope0, slope1)

    def lanes(block):
        return slice(block * LANES, (block + 1) * LANES)

    def span(index):
        return pl.ds(pl.multiple_of(index * step * pair, step * pair), step * pair)

    for block in range(blocks):
        spread(cur_ref[:, lanes(block)].astype(F32), src0, block, height)

    def forward(which):
        def chunk(at, carry):
            block, index = at // chunks, lax.rem(at, chunks)
            act = tap_sum(srcs[which], block, taps_ref, which, index * step, step, False)
            gel, slope = gelu_pair(act.reshape(step * pair, LANES))
            slopes[which][span(index), columns(block)] = slope
            gel_ref[which, span(index), columns(block)] = gel.astype(BF16)
            return carry

        lax.fori_loop(0, blocks * chunks, chunk, 0)
        return jnp.dot(gel_ref[which], point_ref[which], preferred_element_type=F32)

    u_one_ref[...] = forward(0) + cur_ref[...].astype(F32)
    for block in range(blocks):
        spread(u_one_ref[:, lanes(block)], src1, block, height)
    diff = forward(1) + u_one_ref[...] - teach_ref[...].astype(F32)
    resid = diff * (4.0 / rows)
    resid_ref[...] = resid
    grad_ref[1] = resid.astype(BF16)

    def taps_grad(which):
        def over_rows(at, carry):
            block, row = at // 7, lax.rem(at, 7)
            strip = srcs[which][block, row].astype(BF16)
            part = dact[:, columns(block)].reshape(-1, pair, LANES).astype(BF16)
            count = part.shape[0]
            for col in range(7):
                prod = strip[col : col + count] * part
                size = count
                while size > 1:
                    size //= 2
                    prod = prod[:size] + prod[size:]
                line = jnp.sum(prod[0].astype(F32), axis=0, keepdims=True)
                dk_ref[which, block, row, col : col + 1, :] = line
            dk_ref[which, block, row, 7:8, :] = jnp.zeros((1, LANES), F32)
            return carry

        lax.fori_loop(0, 7 * blocks, over_rows, 0)

    def back_point(which):
        dgel = lax.dot_general(grad_ref[which], point_ref[which], NT, preferred_element_type=F32)
        return dgel * slopes[which][...]

    dact_one = back_point(1)
    dact[...] = dact_one
    for block in range(blocks):
        spread(dact_one[:, lanes(block)], src2, block, height)

    def chunk_back(at, carry):
        block, index = at // chunks, lax.rem(at, chunks)
        back = tap_sum(src2, block, taps_ref, 1, index * step, step, True)
        back = back.reshape(step * pair, LANES) + resid_ref[span(index), columns(block)]
        grad_ref[0, span(index), columns(block)] = back.astype(BF16)
        return carry

    lax.fori_loop(0, blocks * chunks, chunk_back, 0)
    taps_grad(1)
    dact[...] = back_point(0)
    taps_grad(0)


def student(current, teach, taps, point, height):
    rows, chans = current.shape
    blocks = chans // LANES
    half = rows // (2 * height)
    vmem = pl.BlockSpec(memory_space=pltpu.VMEM)
    spread_shape = pltpu.VMEM((blocks, 7, half + 6, 2 * height, LANES), F32)
    map_shape = pltpu.VMEM((rows, chans), F32)
    return pl.pallas_call(
        functools.partial(student_kernel, height, half // 2),
        out_shape=(
            jax.ShapeDtypeStruct((2, rows, chans), BF16),
            jax.ShapeDtypeStruct((2, rows, chans), BF16),
            jax.ShapeDtypeStruct((2, blocks, 7, 8, LANES), F32),
        ),
        in_specs=[vmem] * 4,
        out_specs=(vmem,) * 3,
        scratch_shapes=[spread_shape] * 3
        + [map_shape] * 2
        + [map_shape] * 3,
        compiler_params=pltpu.CompilerParams(vmem_limit_bytes=32 << 20),
        cost_estimate=pl.CostEstimate(
            flops=10_000_000_000, bytes_accessed=8 * rows * chans, transcendentals=0
        ),
        name="student",
    )(current, teach, taps, point)


def body(pipe_maps, fresh_maps, teacher_weight, student_depth, student_point):
    _, _, height, width, chans = pipe_maps.shape
    rows = height * width
    blocks = chans // LANES
    lead = (lax.axis_index("section") == 0).astype(jnp.int32).reshape(1)
    sections = lax.axis_size("section")
    route = [(i, i + 1) for i in range(sections - 1)]

    def to_rows(maps):
        front = maps.shape[:-3]
        split = maps.reshape(front + (height, 2, width // 2, chans))
        return jnp.swapaxes(split, -4, -2).reshape(front + (rows, chans))

    relay = to_rows(pipe_maps[0, 0])
    fresh = to_rows(fresh_maps[:, 0])
    weight = teacher_weight.reshape(2, 9 * chans, chans)
    ticks = fresh_maps.shape[0] + 1
    gels, grads, depth_total = [], [], None
    teach = relay
    for tick in range(ticks):
        mine = relay if tick == 0 else fresh[tick - 1]
        teach, current = teacher(lead, mine, relay, weight, height)
        if tick + 1 < ticks:
            relay = lax.ppermute(teach, "section", route)
        gel, grad, part = student(current, teach, student_depth, student_point, height)
        gels.append(gel)
        grads.append(grad)
        depth_total = part if depth_total is None else depth_total + part
    gel_all = jnp.concatenate(gels, axis=1)
    grad_all = jnp.concatenate(grads, axis=1)
    point_total = [
        lax.dot_general(grad_all[b], gel_all[b], (((0,), (0,)), ((), ())), preferred_element_type=F32)
        for b in range(2)
    ]
    depth_rows = depth_total[:, :, :, :7].transpose(1, 4, 0, 2, 3).reshape(chans, 98)
    packed = jnp.concatenate(point_total + [depth_rows], axis=1)
    parties = lax.axis_size("dp")
    share = chans // parties
    me = lax.axis_index("dp")
    total = lax.dynamic_slice_in_dim(packed, me * share, share, 0)
    for hop in range(1, parties):
        out = lax.dynamic_slice_in_dim(packed, lax.rem(me + hop, parties) * share, share, 0)
        pairs = [(i, (i + hop) % parties) for i in range(parties)]
        total = total + lax.ppermute(out.astype(BF16), "dp", pairs).astype(F32)
    point_grad = jnp.stack([total[:, b * chans : (b + 1) * chans].T for b in range(2)])
    depth_grad = total[:, 2 * chans :].T.reshape(2, 49, share)
    final = jnp.swapaxes(teach.reshape(width // 2, 2, height, chans), 0, 2)
    final = final.reshape(1, 1, height, width, chans)
    return final, point_grad, depth_grad


def solution(mesh):
    placed = (
        P("section", "dp", None, None, None),
        P(None, "dp", None, None, None),
        P("section", None, None, None, None),
        P("section", None, None),
        P("section", None, None),
    )
    return jax.shard_map(
        body,
        mesh=mesh,
        in_specs=placed,
        out_specs=(
            P("section", "dp", None, None, None),
            P("section", None, "dp"),
            P("section", None, "dp"),
        ),
        check_vma=False,
    )
```

```python
import functools

import jax
import jax.numpy as jnp
from jax import lax
from jax.experimental import pallas as pl
from jax.experimental.pallas import tpu as pltpu
from jax.sharding import PartitionSpec as P

LANES = 128
F32 = jnp.float32
BF16 = jnp.bfloat16
MESH = pl.DeviceIdType.MESH
NT = (((1,), (1,)), ((), ()))


def gather_windows(vals, win_ref, height):
    rows, chans = vals.shape
    pair = 2 * height
    h_of = lax.rem(lax.broadcasted_iota(jnp.int32, (rows, chans), 0), height)
    zero = jnp.zeros((height, chans), F32)
    cube = vals.reshape(rows // height, height, chans)
    for row in range(3):
        dy = row - 1
        moved = vals
        if dy:
            moved = pltpu.roll(cube, (-dy) % height, 1).reshape(rows, chans)
            moved = jnp.where((h_of + dy >= 0) & (h_of + dy < height), moved, 0.0)
        for col in range(3):
            if col == 0:
                part = jnp.concatenate([zero, moved[rows - pair : rows - height], moved[: rows - pair]], axis=0)
            elif col == 2:
                part = jnp.concatenate([moved[pair:], moved[height:pair], zero], axis=0)
            else:
                part = moved
            tap = row * 3 + col
            win_ref[:, tap * chans : (tap + 1) * chans] = part.astype(BF16)


def teacher_kernel(height, lead_ref, fresh_ref, relay_ref, weight_ref, teach_ref, cur_ref, win_ref):
    lead = lead_ref[0] == 1
    current = jnp.where(lead, fresh_ref[...].astype(F32), relay_ref[...].astype(F32))
    cur_ref[...] = current.astype(BF16)
    gather_windows(current, win_ref, height)
    hidden = jnp.dot(win_ref[...], weight_ref[0], preferred_element_type=F32)
    gather_windows(jnp.maximum(hidden, 0.0), win_ref, height)
    second = jnp.dot(win_ref[...], weight_ref[1], preferred_element_type=F32)
    teach_ref[...] = (0.8 * (current + second)).astype(BF16)


def teacher(lead, fresh, relay, weight, height):
    rows, chans = fresh.shape
    vmem = pl.BlockSpec(memory_space=pltpu.VMEM)
    return pl.pallas_call(
        functools.partial(teacher_kernel, height),
        out_shape=(jax.ShapeDtypeStruct((rows, chans), BF16),) * 2,
        in_specs=[pl.BlockSpec(memory_space=pltpu.SMEM), vmem, vmem, vmem],
        out_specs=(vmem, vmem),
        scratch_shapes=[pltpu.VMEM((rows, 9 * chans), BF16)],
        compiler_params=pltpu.CompilerParams(vmem_limit_bytes=12 << 20),
        cost_estimate=pl.CostEstimate(
            flops=2 * 2 * 9 * rows * chans * chans, bytes_accessed=weight.size * 2, transcendentals=0
        ),
        name="teacher",
    )(lead, fresh, relay, weight)


def spread(vals, out_ref, block, height):
    pair = vals.reshape(-1, 2 * height, LANES)
    low, high = pair[:, :height], pair[:, height:]
    h_of = lax.broadcasted_iota(jnp.int32, low.shape, 1)
    zero = jnp.zeros((3, height, LANES), F32)
    for row in range(7):
        dy = row - 3
        one, two = low, high
        if dy:
            keep = (h_of + dy >= 0) & (h_of + dy < height)
            one = jnp.where(keep, pltpu.roll(low, (-dy) % height, 1), 0.0)
            two = jnp.where(keep, pltpu.roll(high, (-dy) % height, 1), 0.0)
        left = jnp.concatenate([zero, one, two[:3]], axis=0)
        right = jnp.concatenate([one[-3:], two, zero], axis=0)
        out_ref[block, row] = jnp.concatenate([left, right], axis=1)


def columns(block):
    return pl.ds(pl.multiple_of(block * LANES, LANES), LANES)


def tap_sum(src_ref, block, taps_ref, which, start, count, flip):
    total, held = None, None
    for row in range(7):
        strip = src_ref[block, row, pl.ds(start, count + 6)].astype(BF16)
        terms = []
        for col in range(7):
            tap = row * 7 + col
            tap = 48 - tap if flip else tap
            coef = jnp.broadcast_to(taps_ref[which, tap : tap + 1, columns(block)], strip.shape[1:])
            terms.append(strip[col : col + count] * coef.astype(BF16)[None])
        while len(terms) > 1:
            terms = [sum(terms[i + 1 : i + 2], terms[i]) for i in range(0, len(terms), 2)]
        if held is None and row < 6:
            held = terms[0]
            continue
        part = terms[0] if held is None else held + terms[0]
        held = None
        total = part.astype(F32) if total is None else total + part.astype(F32)
    return total


def gelu_pair(act):
    root = 0.7978845608028654
    square = act * act
    tanh = jnp.tanh(root * (act + 0.044715 * square * act))
    half = 0.5 * (1.0 + tanh)
    slope = half + 0.5 * act * (1.0 - tanh * tanh) * (root * (1.0 + 3.0 * 0.044715 * square))
    return act * half, slope


def student_kernel(
    height, step, sections, cur_ref, teach_ref, taps_ref, point_ref,
    gel0, gel1, grad0, grad1, dk_ref, *rest,
):
    if sections:
        relay_ref, *rest = rest
        *rest, land, send_sem, recv_sem = rest
        spot = lax.axis_index("section")
        later, earlier = lax.rem(spot + 1, sections), lax.rem(spot + sections - 1, sections)
        barrier = pltpu.get_barrier_semaphore()

        @pl.when(spot > 0)
        def _():
            pl.semaphore_signal(barrier, inc=1, device_id={"section": earlier}, device_id_type=MESH)

        copy = pltpu.make_async_remote_copy(
            src_ref=teach_ref,
            dst_ref=land,
            send_sem=send_sem,
            recv_sem=recv_sem,
            device_id={"section": later},
            device_id_type=MESH,
        )
    src0, src1, src2, slope0, slope1, dact, u_one_ref, resid_ref = rest
    gels, grads = (gel0, gel1), (grad0, grad1)
    rows, chans = cur_ref.shape
    blocks = chans // LANES
    pair = 2 * height
    chunks = rows // (pair * step)
    srcs, slopes = (src0, src1), (slope0, slope1)

    def lanes(block):
        return slice(block * LANES, (block + 1) * LANES)

    def span(index):
        return pl.ds(pl.multiple_of(index * step * pair, step * pair), step * pair)

    for block in range(blocks):
        spread(cur_ref[:, lanes(block)].astype(F32), src0, block, height)

    def forward(which):
        def chunk(at, carry):
            block, index = at // chunks, lax.rem(at, chunks)
            act = tap_sum(srcs[which], block, taps_ref, which, index * step, step, False)
            gel, slope = gelu_pair(act.reshape(step * pair, LANES))
            slopes[which][span(index), columns(block)] = slope
            gels[which][span(index), columns(block)] = gel.astype(BF16)
            return carry

        lax.fori_loop(0, blocks * chunks, chunk, 0)
        return jnp.dot(gels[which][...], point_ref[which], preferred_element_type=F32)

    u_one_ref[...] = forward(0) + cur_ref[...].astype(F32)
    for block in range(blocks):
        spread(u_one_ref[:, lanes(block)], src1, block, height)
    if sections:

        @pl.when(spot < sections - 1)
        def _():
            pl.semaphore_wait(barrier, 1)
            copy.start()

    diff = forward(1) + u_one_ref[...] - teach_ref[...].astype(F32)
    resid = diff * (4.0 / rows)
    resid_ref[...] = resid
    grad1[...] = resid.astype(BF16)

    def taps_grad(which):
        def over_rows(at, carry):
            block, row = at // 7, lax.rem(at, 7)
            strip = srcs[which][block, row].astype(BF16)
            part = dact[:, columns(block)].reshape(-1, pair, LANES).astype(BF16)
            count = part.shape[0]
            for col in range(7):
                prod = strip[col : col + count] * part
                size = count
                while size > 1:
                    size //= 2
                    prod = prod[:size] + prod[size:]
                line = jnp.sum(prod[0].astype(F32), axis=0, keepdims=True)
                dk_ref[which, block, row, col : col + 1, :] = line
            dk_ref[which, block, row, 7:8, :] = jnp.zeros((1, LANES), F32)
            return carry

        lax.fori_loop(0, 7 * blocks, over_rows, 0)

    def back_point(which):
        dgel = lax.dot_general(grads[which][...], point_ref[which], NT, preferred_element_type=F32)
        return dgel * slopes[which][...]

    dact_one = back_point(1)
    dact[...] = dact_one
    for block in range(blocks):
        spread(dact_one[:, lanes(block)], src2, block, height)

    def chunk_back(at, carry):
        block, index = at // chunks, lax.rem(at, chunks)
        back = tap_sum(src2, block, taps_ref, 1, index * step, step, True)
        back = back.reshape(step * pair, LANES) + resid_ref[span(index), columns(block)]
        grad0[span(index), columns(block)] = back.astype(BF16)
        return carry

    lax.fori_loop(0, blocks * chunks, chunk_back, 0)
    taps_grad(1)
    dact[...] = back_point(0)
    taps_grad(0)
    if sections:

        @pl.when(spot > 0)
        def _():
            copy.wait_recv()
            relay_ref[...] = land[...]

        @pl.when(spot == 0)
        def _():
            relay_ref[...] = jnp.zeros_like(relay_ref)

        @pl.when(spot < sections - 1)
        def _():
            copy.wait_send()


def student(current, teach, taps, point, height, sections):
    rows, chans = current.shape
    blocks = chans // LANES
    half = rows // (2 * height)
    vmem = pl.BlockSpec(memory_space=pltpu.VMEM)
    spread_shape = pltpu.VMEM((blocks, 7, half + 6, 2 * height, LANES), F32)
    map_shape = pltpu.VMEM((rows, chans), F32)
    flat = jax.ShapeDtypeStruct((rows, chans), BF16)
    outs = [flat] * 4 + [jax.ShapeDtypeStruct((2, blocks, 7, 8, LANES), F32)]
    scratch = [spread_shape] * 3 + [map_shape] * 5
    params = {}
    if sections:
        outs.append(flat)
        scratch += [pltpu.VMEM((rows, chans), BF16), pltpu.SemaphoreType.DMA, pltpu.SemaphoreType.DMA]
        params = {"collective_id": 0, "has_side_effects": True}
    return pl.pallas_call(
        functools.partial(student_kernel, height, half // 2, sections),
        out_shape=tuple(outs),
        in_specs=[vmem] * 4,
        out_specs=(vmem,) * len(outs),
        scratch_shapes=scratch,
        compiler_params=pltpu.CompilerParams(vmem_limit_bytes=22 << 20, **params),
        cost_estimate=pl.CostEstimate(
            flops=10_000_000_000, bytes_accessed=8 * rows * chans, transcendentals=0
        ),
        name="student",
    )(current, teach, taps, point)


def body(pipe_maps, fresh_maps, teacher_weight, student_depth, student_point):
    _, _, height, width, chans = pipe_maps.shape
    rows = height * width
    blocks = chans // LANES
    lead = (lax.axis_index("section") == 0).astype(jnp.int32).reshape(1)
    sections = lax.axis_size("section")

    def to_rows(maps):
        front = maps.shape[:-3]
        split = maps.reshape(front + (height, 2, width // 2, chans))
        return jnp.swapaxes(split, -4, -2).reshape(front + (rows, chans))

    relay = to_rows(pipe_maps[0, 0])
    fresh = to_rows(fresh_maps[:, 0])
    weight = teacher_weight.reshape(2, 9 * chans, chans)
    ticks = fresh_maps.shape[0] + 1
    gels, grads, depth_total = [], [], None
    teach = relay
    for tick in range(ticks):
        mine = relay if tick == 0 else fresh[tick - 1]
        teach, current = teacher(lead, mine, relay, weight, height)
        linked = sections if tick + 1 < ticks else 0
        gel0, gel1, grad0, grad1, part, *sent = student(
            current, teach, student_depth, student_point, height, linked
        )
        if sent:
            relay = sent[0]
        gels.append((gel0, gel1))
        grads.append((grad0, grad1))
        depth_total = part if depth_total is None else depth_total + part
    gel_all = [jnp.concatenate([pair[b] for pair in gels]) for b in range(2)]
    grad_all = [jnp.concatenate([pair[b] for pair in grads]) for b in range(2)]
    point_total = [
        lax.dot_general(grad_all[b], gel_all[b], (((0,), (0,)), ((), ())), preferred_element_type=F32)
        for b in range(2)
    ]
    depth_rows = depth_total[:, :, :, :7].transpose(1, 4, 0, 2, 3).reshape(chans, 98)
    packed = jnp.concatenate(point_total + [depth_rows], axis=1)
    parties = lax.axis_size("dp")
    share = chans // parties
    me = lax.axis_index("dp")
    total = lax.dynamic_slice_in_dim(packed, me * share, share, 0)
    for hop in range(1, parties):
        out = lax.dynamic_slice_in_dim(packed, lax.rem(me + hop, parties) * share, share, 0)
        pairs = [(i, (i + hop) % parties) for i in range(parties)]
        total = total + lax.ppermute(out.astype(BF16), "dp", pairs).astype(F32)
    point_grad = jnp.stack([total[:, b * chans : (b + 1) * chans].T for b in range(2)])
    depth_grad = total[:, 2 * chans :].T.reshape(2, 49, share)
    final = jnp.swapaxes(teach.reshape(width // 2, 2, height, chans), 0, 2)
    final = final.reshape(1, 1, height, width, chans)
    return final, point_grad, depth_grad


def solution(mesh):
    placed = (
        P("section", "dp", None, None, None),
        P(None, "dp", None, None, None),
        P("section", None, None, None, None),
        P("section", None, None),
        P("section", None, None),
    )
    return jax.shard_map(
        body,
        mesh=mesh,
        in_specs=placed,
        out_specs=(
            P("section", "dp", None, None, None),
            P("section", None, "dp"),
            P("section", None, "dp"),
        ),
        check_vma=False,
    )
```

```python
import functools

import jax
import jax.numpy as jnp
from jax import lax
from jax.experimental import pallas as pl
from jax.experimental.pallas import tpu as pltpu
from jax.sharding import PartitionSpec as P

LANES = 128
F32 = jnp.float32
BF16 = jnp.bfloat16
MESH = pl.DeviceIdType.MESH
NT = (((1,), (1,)), ((), ()))


def gather_windows(vals, win_ref, height):
    rows, chans = vals.shape
    pair = 2 * height
    h_of = lax.rem(lax.broadcasted_iota(jnp.int32, (rows, chans), 0), height)
    zero = jnp.zeros((height, chans), F32)
    cube = vals.reshape(rows // height, height, chans)
    for row in range(3):
        dy = row - 1
        moved = vals
        if dy:
            moved = pltpu.roll(cube, (-dy) % height, 1).reshape(rows, chans)
            moved = jnp.where((h_of + dy >= 0) & (h_of + dy < height), moved, 0.0)
        for col in range(3):
            if col == 0:
                part = jnp.concatenate([zero, moved[rows - pair : rows - height], moved[: rows - pair]], axis=0)
            elif col == 2:
                part = jnp.concatenate([moved[pair:], moved[height:pair], zero], axis=0)
            else:
                part = moved
            tap = row * 3 + col
            win_ref[:, tap * chans : (tap + 1) * chans] = part.astype(BF16)


def teacher_kernel(height, lead_ref, fresh_ref, relay_ref, weight_ref, teach_ref, cur_ref, win_ref):
    lead = lead_ref[0] == 1
    current = jnp.where(lead, fresh_ref[...].astype(F32), relay_ref[...].astype(F32))
    cur_ref[...] = current.astype(BF16)
    gather_windows(current, win_ref, height)
    hidden = jnp.dot(win_ref[...], weight_ref[0], preferred_element_type=F32)
    gather_windows(jnp.maximum(hidden, 0.0), win_ref, height)
    second = jnp.dot(win_ref[...], weight_ref[1], preferred_element_type=F32)
    teach_ref[...] = (0.8 * (current + second)).astype(BF16)


def teacher(lead, fresh, relay, weight, height):
    rows, chans = fresh.shape
    vmem = pl.BlockSpec(memory_space=pltpu.VMEM)
    return pl.pallas_call(
        functools.partial(teacher_kernel, height),
        out_shape=(jax.ShapeDtypeStruct((rows, chans), BF16),) * 2,
        in_specs=[pl.BlockSpec(memory_space=pltpu.SMEM), vmem, vmem, vmem],
        out_specs=(vmem, vmem),
        scratch_shapes=[pltpu.VMEM((rows, 9 * chans), BF16)],
        compiler_params=pltpu.CompilerParams(vmem_limit_bytes=12 << 20),
        cost_estimate=pl.CostEstimate(
            flops=2 * 2 * 9 * rows * chans * chans, bytes_accessed=weight.size * 2, transcendentals=0
        ),
        name="teacher",
    )(lead, fresh, relay, weight)


def spread(vals, out_ref, block, height):
    pair = vals.reshape(-1, 2 * height, LANES)
    low, high = pair[:, :height], pair[:, height:]
    h_of = lax.broadcasted_iota(jnp.int32, low.shape, 1)
    zero = jnp.zeros((3, height, LANES), F32)
    for row in range(7):
        dy = row - 3
        one, two = low, high
        if dy:
            keep = (h_of + dy >= 0) & (h_of + dy < height)
            one = jnp.where(keep, pltpu.roll(low, (-dy) % height, 1), 0.0)
            two = jnp.where(keep, pltpu.roll(high, (-dy) % height, 1), 0.0)
        left = jnp.concatenate([zero, one, two[:3]], axis=0)
        right = jnp.concatenate([one[-3:], two, zero], axis=0)
        out_ref[block, row] = jnp.concatenate([left, right], axis=1)


def columns(block):
    return pl.ds(pl.multiple_of(block * LANES, LANES), LANES)


def tap_sum(src_ref, block, taps_ref, which, start, count, flip):
    total, held = None, None
    for row in range(7):
        strip = src_ref[block, row, pl.ds(start, count + 6)].astype(BF16)
        terms = []
        for col in range(7):
            tap = row * 7 + col
            tap = 48 - tap if flip else tap
            coef = jnp.broadcast_to(taps_ref[which, tap : tap + 1, columns(block)], strip.shape[1:])
            terms.append(strip[col : col + count] * coef.astype(BF16)[None])
        while len(terms) > 1:
            terms = [sum(terms[i + 1 : i + 2], terms[i]) for i in range(0, len(terms), 2)]
        if held is None and row < 6:
            held = terms[0]
            continue
        part = terms[0] if held is None else held + terms[0]
        held = None
        total = part.astype(F32) if total is None else total + part.astype(F32)
    return total


def gelu_pair(act):
    root = 0.7978845608028654
    square = act * act
    tanh = jnp.tanh(root * (act + 0.044715 * square * act))
    half = 0.5 * (1.0 + tanh)
    slope = half + 0.5 * act * (1.0 - tanh * tanh) * (root * (1.0 + 3.0 * 0.044715 * square))
    return act * half, slope


def student_kernel(
    height, step, sections, cur_ref, teach_ref, taps_ref, point_ref,
    gel0, gel1, grad0, grad1, dk_ref, *rest,
):
    if sections:
        relay_ref, *rest = rest
        *rest, land, send_sem, recv_sem = rest
        spot = lax.axis_index("section")
        later, earlier = lax.rem(spot + 1, sections), lax.rem(spot + sections - 1, sections)
        barrier = pltpu.get_barrier_semaphore()

        @pl.when(spot > 0)
        def _():
            pl.semaphore_signal(barrier, inc=1, device_id={"section": earlier}, device_id_type=MESH)

        copy = pltpu.make_async_remote_copy(
            src_ref=teach_ref,
            dst_ref=land,
            send_sem=send_sem,
            recv_sem=recv_sem,
            device_id={"section": later},
            device_id_type=MESH,
        )
    src0, src1, src2, slope0, slope1, dact, u_one_ref, resid_ref, sums_ref = rest
    gels, grads = (gel0, gel1), (grad0, grad1)
    rows, chans = cur_ref.shape
    blocks = chans // LANES
    pair = 2 * height
    chunks = rows // (pair * step)
    srcs, slopes = (src0, src1), (slope0, slope1)

    def lanes(block):
        return slice(block * LANES, (block + 1) * LANES)

    def span(index):
        return pl.ds(pl.multiple_of(index * step * pair, step * pair), step * pair)

    for block in range(blocks):
        spread(cur_ref[:, lanes(block)].astype(F32), src0, block, height)

    def forward(which):
        def chunk(at, carry):
            block, index = at // chunks, lax.rem(at, chunks)
            act = tap_sum(srcs[which], block, taps_ref, which, index * step, step, False)
            gel, slope = gelu_pair(act.reshape(step * pair, LANES))
            slopes[which][span(index), columns(block)] = slope
            gels[which][span(index), columns(block)] = gel.astype(BF16)
            return carry

        lax.fori_loop(0, blocks * chunks, chunk, 0)
        return jnp.dot(gels[which][...], point_ref[which], preferred_element_type=F32)

    u_one_ref[...] = forward(0) + cur_ref[...].astype(F32)
    for block in range(blocks):
        spread(u_one_ref[:, lanes(block)], src1, block, height)
    if sections:

        @pl.when(spot < sections - 1)
        def _():
            pl.semaphore_wait(barrier, 1)
            copy.start()

    diff = forward(1) + u_one_ref[...] - teach_ref[...].astype(F32)
    resid = diff * (4.0 / rows)
    resid_ref[...] = resid
    grad1[...] = resid.astype(BF16)

    def taps_grad(which):
        def over_rows(at, carry):
            block, row = at // 7, lax.rem(at, 7)
            strip = srcs[which][block, row].astype(BF16)
            part = dact[:, columns(block)].reshape(-1, pair, LANES).astype(BF16)
            count = part.shape[0]
            for col in range(7):
                prod = strip[col : col + count] * part
                size = count
                while size > 1:
                    size //= 2
                    prod = prod[:size] + prod[size:]
                wide = prod[0].astype(F32)
                sums_ref[block, row, col] = wide[:height] + wide[height:]
            return carry

        lax.fori_loop(0, 7 * blocks, over_rows, 0)
        for block in range(blocks):
            for row in range(7):
                dk_ref[which, block, row] = jnp.sum(sums_ref[block, row], axis=1)

    def back_point(which):
        dgel = lax.dot_general(grads[which][...], point_ref[which], NT, preferred_element_type=F32)
        return dgel * slopes[which][...]

    dact_one = back_point(1)
    dact[...] = dact_one
    for block in range(blocks):
        spread(dact_one[:, lanes(block)], src2, block, height)

    def chunk_back(at, carry):
        block, index = at // chunks, lax.rem(at, chunks)
        back = tap_sum(src2, block, taps_ref, 1, index * step, step, True)
        back = back.reshape(step * pair, LANES) + resid_ref[span(index), columns(block)]
        grad0[span(index), columns(block)] = back.astype(BF16)
        return carry

    lax.fori_loop(0, blocks * chunks, chunk_back, 0)
    taps_grad(1)
    dact[...] = back_point(0)
    taps_grad(0)
    if sections:

        @pl.when(spot > 0)
        def _():
            copy.wait_recv()
            relay_ref[...] = land[...]

        @pl.when(spot == 0)
        def _():
            relay_ref[...] = jnp.zeros_like(relay_ref)

        @pl.when(spot < sections - 1)
        def _():
            copy.wait_send()


def student(current, teach, taps, point, height, sections):
    rows, chans = current.shape
    blocks = chans // LANES
    half = rows // (2 * height)
    vmem = pl.BlockSpec(memory_space=pltpu.VMEM)
    spread_shape = pltpu.VMEM((blocks, 7, half + 6, 2 * height, LANES), F32)
    map_shape = pltpu.VMEM((rows, chans), F32)
    flat = jax.ShapeDtypeStruct((rows, chans), BF16)
    outs = [flat] * 4 + [jax.ShapeDtypeStruct((2, blocks, 7, 7, LANES), F32)]
    scratch = [spread_shape] * 3 + [map_shape] * 5 + [pltpu.VMEM((blocks, 7, 7, height, LANES), F32)]
    params = {}
    if sections:
        outs.append(flat)
        scratch += [pltpu.VMEM((rows, chans), BF16), pltpu.SemaphoreType.DMA, pltpu.SemaphoreType.DMA]
        params = {"collective_id": 0, "has_side_effects": True}
    return pl.pallas_call(
        functools.partial(student_kernel, height, half // 2, sections),
        out_shape=tuple(outs),
        in_specs=[vmem] * 4,
        out_specs=(vmem,) * len(outs),
        scratch_shapes=scratch,
        compiler_params=pltpu.CompilerParams(vmem_limit_bytes=22 << 20, **params),
        cost_estimate=pl.CostEstimate(
            flops=10_000_000_000, bytes_accessed=8 * rows * chans, transcendentals=0
        ),
        name="student",
    )(current, teach, taps, point)


def body(pipe_maps, fresh_maps, teacher_weight, student_depth, student_point):
    _, _, height, width, chans = pipe_maps.shape
    rows = height * width
    blocks = chans // LANES
    lead = (lax.axis_index("section") == 0).astype(jnp.int32).reshape(1)
    sections = lax.axis_size("section")

    def to_rows(maps):
        front = maps.shape[:-3]
        split = maps.reshape(front + (height, 2, width // 2, chans))
        return jnp.swapaxes(split, -4, -2).reshape(front + (rows, chans))

    relay = to_rows(pipe_maps[0, 0])
    fresh = to_rows(fresh_maps[:, 0])
    weight = teacher_weight.reshape(2, 9 * chans, chans)
    ticks = fresh_maps.shape[0] + 1
    gels, grads, depth_total = [], [], None
    teach = relay
    for tick in range(ticks):
        mine = relay if tick == 0 else fresh[tick - 1]
        teach, current = teacher(lead, mine, relay, weight, height)
        linked = sections if tick + 1 < ticks else 0
        gel0, gel1, grad0, grad1, part, *sent = student(
            current, teach, student_depth, student_point, height, linked
        )
        if sent:
            relay = sent[0]
        gels.append((gel0, gel1))
        grads.append((grad0, grad1))
        depth_total = part if depth_total is None else depth_total + part
    gel_all = [jnp.concatenate([pair[b] for pair in gels]) for b in range(2)]
    grad_all = [jnp.concatenate([pair[b] for pair in grads]) for b in range(2)]
    point_total = [
        lax.dot_general(grad_all[b], gel_all[b], (((0,), (0,)), ((), ())), preferred_element_type=F32)
        for b in range(2)
    ]
    depth_rows = depth_total.transpose(1, 4, 0, 2, 3).reshape(chans, 98)
    packed = jnp.concatenate(point_total + [depth_rows], axis=1)
    parties = lax.axis_size("dp")
    share = chans // parties
    me = lax.axis_index("dp")
    total = lax.dynamic_slice_in_dim(packed, me * share, share, 0)
    for hop in range(1, parties):
        out = lax.dynamic_slice_in_dim(packed, lax.rem(me + hop, parties) * share, share, 0)
        pairs = [(i, (i + hop) % parties) for i in range(parties)]
        total = total + lax.ppermute(out.astype(BF16), "dp", pairs).astype(F32)
    point_grad = jnp.stack([total[:, b * chans : (b + 1) * chans] for b in range(2)]).swapaxes(1, 2)
    depth_grad = total[:, 2 * chans :].T.reshape(2, 49, share)
    final = jnp.swapaxes(teach.reshape(width // 2, 2, height, chans), 0, 2)
    final = final.reshape(1, 1, height, width, chans)
    return final, point_grad, depth_grad


def solution(mesh):
    placed = (
        P("section", "dp", None, None, None),
        P(None, "dp", None, None, None),
        P("section", None, None, None, None),
        P("section", None, None),
        P("section", None, None),
    )
    return jax.shard_map(
        body,
        mesh=mesh,
        in_specs=placed,
        out_specs=(
            P("section", "dp", None, None, None),
            P("section", None, "dp"),
            P("section", None, "dp"),
        ),
        check_vma=False,
    )
```
